32 devices in a mesh: loop: 8 (over y, x, core), rep: 4 (over z).
Axes of the slice: x: 2, y: 2, z: 4, core: 2. Of those that a mesh axis runs over, the one named last changes fastest.
Arguments:
- features: bfloat16 [8192, 512], P(('loop', 'rep')), may hold values from -6 to 6
- tiles: bfloat16 [2560, 128, 128], P(('loop', 'rep')), may hold values from -0.59765625 to 0.59765625
- slot_tile_row: int32 [2560], P(('loop', 'rep')), may hold values from 0 to 7
- slot_tile_column: int32 [2560], P(('loop', 'rep')), may hold values from 0 to 1
- counts: int32 [160], P(('loop', 'rep')), may hold values from 1 to 16, as said below
- degree: int32 [8192], P(('loop', 'rep')), may hold values from 1 to 8
- w_self: bfloat16 [512, 512], replicated, may hold values from -0.25 to 0.25
- w_neigh: bfloat16 [512, 512], replicated, may hold values from -0.25 to 0.25
Outputs:
- updated: bfloat16 [8192, 512], P(('loop', 'rep'))
The draws below stay inside these ranges and needn't reach their ends.
Inputs may be any that keep to these rules, and one draw needn't show every extreme that they name: `counts`: each group has at least one live slot, and in every draw some group has all 16 slots live.
All inputs are finite; a program needn't handle non-finite values.
Results may differ from the reference program's by a relative error of at most 0.0045.
Values may be sent and summed in bfloat16 or wider, within the bound.
No kernel may reach another device: no remote copies, remote signals or barrier semaphores. Data moves between devices by JAX's collectives and lax.ppermute only.
A program may use at most 128 MiB of HBM per device.

```python
import jax
import jax.numpy as jnp
from jax import lax

H = 512
TILE_WIDTH = 128
DEVICE_NODES = 256
CAP = 16
SPAN = 2
STEPS = 5
BLOCK_TILE_ROWS = 8
NODES = 8192
SLOT_COUNT = 2560
NCOUNT = 160
N_LOOP = 8
N_REP = 4


def draw_counts(key, part):
    first, second, third = jax.random.split(jax.random.fold_in(key, 17), 3)
    upper = jax.random.randint(first, (NCOUNT,), 0, CAP + 1)
    lower = jax.random.randint(second, (NCOUNT,), 0, CAP + 1)
    values = jnp.minimum(1 + upper * lower // CAP, CAP)
    chosen = jax.random.randint(third, (), 0, NCOUNT)
    return jnp.where(jnp.arange(NCOUNT) == chosen, CAP, values).astype(jnp.int32)


def plant(result, rng, smallest, high):
    longest = result.shape.index(max(result.shape))
    spots = []
    for shift in (0, 1):
        where = [jax.random.randint(jax.random.fold_in(rng, axis), (), 0, length) for axis, length in enumerate(result.shape)]
        where[longest] = (where[longest] + shift) % result.shape[longest]
        spots.append(tuple(where))
    return result.at[spots[0]].set(smallest).at[spots[1]].set(high)


def shard_levels(key, extent, cuts, least, top_value):
    def one(position, blocks):
        heights = jax.random.uniform(jax.random.fold_in(jax.random.fold_in(key, 6), position), (blocks,), jnp.float32, least / len(cuts), top_value / len(cuts))
        return jnp.repeat(jnp.exp(heights), extent[position] // blocks).reshape((-1,) + (1,) * (len(extent) - position - 1))

    factor_of = one(*cuts[0])
    for cut in cuts[1:]:
        factor_of = factor_of * one(*cut)
    return factor_of


def gaussian(rng, dims, spread, bound, cuts=(), held_as=jnp.bfloat16):
    factor_of = shard_levels(rng, dims, cuts, -0.22, 0.18) if cuts else 1.0
    array = jax.random.normal(rng, dims, jnp.float32) * spread * factor_of
    return jnp.minimum(jnp.maximum(array, -bound), bound).astype(held_as)


def setup_inputs(seed: int = 0) -> dict:
    seeds = jax.random.split(jax.random.key(seed), 9)
    return {
        "features": gaussian(seeds[0], (NODES, H), 1.0, 6.0, ((0, 32),)),
        "tiles": gaussian(seeds[1], (SLOT_COUNT, TILE_WIDTH, TILE_WIDTH), 0.1, 0.59765625, ((0, 32),)),
        "slot_tile_row": plant(jax.random.randint(seeds[2], (SLOT_COUNT,), 0, BLOCK_TILE_ROWS), jax.random.fold_in(seeds[2], 1), 0, BLOCK_TILE_ROWS - 1).astype(jnp.int32),
        "slot_tile_column": plant(jax.random.randint(seeds[3], (SLOT_COUNT,), 0, DEVICE_NODES // TILE_WIDTH), jax.random.fold_in(seeds[3], 1), 0, (DEVICE_NODES // TILE_WIDTH) - 1).astype(jnp.int32),
        "counts": draw_counts(jax.random.fold_in(seeds[8], 71), 0),
        "degree": plant(jax.random.randint(seeds[5], (NODES,), 1, 9), jax.random.fold_in(seeds[5], 1), 1, 8).astype(jnp.int32),
        "w_self": gaussian(seeds[6], (H, H), H ** -0.5, 0.25),
        "w_neigh": gaussian(seeds[7], (H, H), H ** -0.5, 0.25),
    }


def reference(features, tiles, slot_tile_row, slot_tile_column, counts, degree, w_self, w_neigh):
    ncol = DEVICE_NODES // TILE_WIDTH
    node_row_blocks = DEVICE_NODES * N_REP // TILE_WIDTH
    feat = features.reshape(N_LOOP, N_REP, ncol, TILE_WIDTH, H)
    tile_all = tiles.reshape(N_LOOP, N_REP, STEPS, CAP, TILE_WIDTH, TILE_WIDTH)
    rows_all = slot_tile_row.reshape(N_LOOP, N_REP, STEPS, CAP)
    cols_all = slot_tile_column.reshape(N_LOOP, N_REP, STEPS, CAP)
    count_all = counts.reshape(N_LOOP, N_REP, STEPS)
    slot_ids = jnp.arange(CAP, dtype=jnp.int32)
    block_ids = jnp.arange(node_row_blocks, dtype=jnp.int32)

    def one_block(index):
        total = jnp.zeros((node_row_blocks, TILE_WIDTH, H), jnp.float32)
        for rep in range(N_REP):
            for step in range(STEPS):
                source_block = (index + step - SPAN) % N_LOOP
                source = feat[source_block, rep]
                picked = jnp.take(source, cols_all[index, rep, step], axis=0).astype(jnp.float32)
                weights = tile_all[index, rep, step].astype(jnp.float32)
                prod = jnp.einsum("cab,cbh->cah", weights, picked, precision=lax.Precision.HIGHEST)
                live = slot_ids < count_all[index, rep, step]
                indicator_matrix = ((rows_all[index, rep, step][None, :] == block_ids[:, None]) & live[None, :]).astype(jnp.float32)
                total = total + jnp.einsum("pc,cah->pah", indicator_matrix, prod, precision=lax.Precision.HIGHEST)
        return total

    summed = lax.map(one_block, jnp.arange(N_LOOP, dtype=jnp.int32)).reshape(NODES, H)
    mean = (summed / degree.astype(jnp.float32)[:, None]).astype(jnp.bfloat16)
    both = jnp.dot(features, w_self, preferred_element_type=jnp.float32) + jnp.dot(mean, w_neigh, preferred_element_type=jnp.float32)
    return jnp.maximum(both, 0.0).astype(jnp.bfloat16)
```

```python
import functools

import jax
import jax.numpy as jnp
from jax import lax
from jax.experimental import pallas as pl
from jax.experimental.pallas import tpu as pltpu
from jax.sharding import PartitionSpec as P

HIDDEN_PARTS = 2
PANEL_ROWS = 8


def permuted(value, axis, pairs):
    return lax.ppermute(value, axis, pairs)


def shift_pairs(count, steps):
    return [(source, (source + steps) % count) for source in range(count)]


def place_of_step(step, span, parity):
    near = jnp.where(step == span + 1, parity == 0, parity == 1)
    place = jnp.where(near, 1, 4)
    place = jnp.where(step == span, 0, place)
    place = jnp.where(step == span + 2, 2, place)
    return jnp.where(step == span - 2, 3, place)


def dense_kernel(steps, capacity, ncol, panel, rows_ref, cols_ref, counts_ref, tiles_ref, out_ref, acc_ref):
    parity = lax.rem(lax.axis_index("loop"), 2)
    first = pl.program_id(0) * panel
    tile = tiles_ref.shape[1]
    acc_ref[...] = jnp.zeros_like(acc_ref)
    for step in range(steps):
        place = place_of_step(step, steps // 2, parity)

        def add(c, carry, step=step, place=place):
            s = step * capacity + c
            p = rows_ref[s] - first

            @pl.when((p >= 0) & (p < panel))
            def _():
                spot = p * (steps * ncol) + place * ncol + cols_ref[s]
                acc_ref[spot] += tiles_ref[s].astype(jnp.float32)

            return carry

        lax.fori_loop(0, counts_ref[step], add, 0)
    for p in range(panel):
        for c in range(steps * ncol):
            out_ref[p * tile : (p + 1) * tile, c * tile : (c + 1) * tile] = acc_ref[p * (steps * ncol) + c].astype(
                out_ref.dtype
            )


def dense_adjacency(tiles, rows, cols, counts, ncol, row_blocks):
    slots, tile, _ = tiles.shape
    steps = counts.shape[0]
    panel = min(PANEL_ROWS, row_blocks)
    width = steps * ncol * tile
    return pl.pallas_call(
        functools.partial(dense_kernel, steps, slots // steps, ncol, panel),
        out_shape=jax.ShapeDtypeStruct((row_blocks * tile, width), jnp.bfloat16),
        grid_spec=pltpu.PrefetchScalarGridSpec(
            num_scalar_prefetch=3,
            grid=(row_blocks // panel,),
            in_specs=[pl.BlockSpec((slots, tile, tile), lambda g, *_: (0, 0, 0))],
            out_specs=pl.BlockSpec((panel * tile, width), lambda g, *_: (g, 0)),
            scratch_shapes=[pltpu.VMEM((panel * steps * ncol, tile, tile), jnp.float32)],
        ),
        cost_estimate=pl.CostEstimate(flops=0, bytes_accessed=3 * 2**21, transcendentals=0),
        name="dense",
    )(rows, cols, counts, tiles)


def product_kernel(count, *refs):
    adj_ref, own_ref, sib_ref, plus_ref, minus_ref, up_ref, down_ref = refs[:7]
    out_refs = refs[7 : 7 + count]
    src_ref = refs[7 + count]
    rows = own_ref.shape[0]
    parity = lax.rem(lax.axis_index("loop"), 2)
    rank = lax.axis_index("rep")
    for place, ref in enumerate((own_ref, sib_ref, plus_ref, minus_ref)):
        src_ref[place * rows : (place + 1) * rows, :] = ref[...]

    @pl.when(parity == 0)
    def _():
        src_ref[4 * rows : 5 * rows, :] = down_ref[...]

    @pl.when(parity == 1)
    def _():
        src_ref[4 * rows : 5 * rows, :] = up_ref[...]

    for ahead in range(count - 1, -1, -1):
        chunk = lax.rem(rank + ahead, count)
        block = adj_ref[pl.ds(pl.multiple_of(chunk * rows, rows), rows), :]
        out_refs[ahead][...] = jnp.dot(block, src_ref[...], preferred_element_type=jnp.float32).astype(
            out_refs[ahead].dtype
        )


def products(adjacency, sources, count):
    rows, width = sources[0].shape
    full = pl.BlockSpec(memory_space=pltpu.VMEM)
    shapes = [jax.ShapeDtypeStruct((rows, width), jnp.float32 if a == 0 else jnp.bfloat16) for a in range(count)]
    return pl.pallas_call(
        functools.partial(product_kernel, count),
        out_shape=shapes,
        in_specs=[full] * (1 + len(sources)),
        out_specs=[full] * count,
        scratch_shapes=[pltpu.VMEM((adjacency.shape[1], width), jnp.bfloat16)],
        cost_estimate=pl.CostEstimate(
            flops=2 * adjacency.shape[0] * adjacency.shape[1] * width, bytes_accessed=2**22, transcendentals=0
        ),
        name="products",
    )(adjacency, *sources)


def finish_kernel(parts, count, *refs):
    sums = refs[: parts * count]
    degree_ref, feat_ref, self_ref, neigh_ref, out_ref = refs[parts * count :]
    degree = degree_ref[...].astype(jnp.float32)
    both = jnp.dot(feat_ref[...], self_ref[...], preferred_element_type=jnp.float32)
    width = sums[0].shape[1]
    for part in range(parts):
        total = sums[part * count][...]
        for other in range(1, count):
            total = total + sums[part * count + other][...].astype(jnp.float32)
        mean = (total / degree).astype(jnp.bfloat16)
        both = both + jnp.dot(
            mean, neigh_ref[part * width : (part + 1) * width, :], preferred_element_type=jnp.float32
        )
    out_ref[...] = jnp.maximum(both, 0.0).astype(out_ref.dtype)


def finish(sums, degree, features, w_self, w_neigh):
    parts, count = len(sums), len(sums[0])
    flat = [value for part in sums for value in part]
    full = pl.BlockSpec(memory_space=pltpu.VMEM)
    return pl.pallas_call(
        functools.partial(finish_kernel, parts, count),
        out_shape=jax.ShapeDtypeStruct(features.shape, features.dtype),
        in_specs=[full] * (len(flat) + 4),
        out_specs=full,
        name="finish",
    )(*flat, degree[:, None], features, w_self, w_neigh)


def shards(features, tiles, slot_tile_row, slot_tile_column, counts, degree, w_self, w_neigh):
    rows_dev, hidden = features.shape
    tile = tiles.shape[1]
    ring = lax.axis_size("loop")
    count = lax.axis_size("rep")
    ncol = rows_dev // tile
    row_blocks = rows_dev * count // tile
    parts = HIDDEN_PARTS
    width = hidden // parts
    ahead, behind = shift_pairs(ring, -2), shift_pairs(ring, 2)
    swap = [(i, i ^ 1) for i in range(ring)]
    up = [(i, i ^ 1) for i in range(0, ring, 2)]
    down = [(i, i ^ 1) for i in range(1, ring, 2)]
    sources = []
    for part in range(parts):
        own = features[:, part * width : (part + 1) * width]
        plus = permuted(own, "loop", ahead)
        minus = permuted(own, "loop", behind)
        sib = permuted(own, "loop", swap)
        relay_up = permuted(plus, "loop", up)
        relay_down = permuted(minus, "loop", down)
        sources.append((own, sib, plus, minus, relay_up, relay_down))
    adjacency = dense_adjacency(tiles, slot_tile_row, slot_tile_column, counts, ncol, row_blocks)
    sums = []
    if count <= 4:
        for part in range(parts):
            terms = products(adjacency, sources[part], count)
            sums.append(
                [terms[0]] + [permuted(terms[s], "rep", shift_pairs(count, s)) for s in range(1, count)]
            )
    else:
        parity = lax.axis_index("loop") % 2
        for own, sib, plus, minus, relay_up, relay_down in sources:
            relayed = jnp.where(parity == 0, relay_down, relay_up)
            stacked = jnp.concatenate((own, sib, plus, minus, relayed), axis=0)
            partial_sum = jnp.dot(adjacency, stacked, preferred_element_type=jnp.float32)
            sums.append([lax.psum_scatter(partial_sum, "rep", scatter_dimension=0, tiled=True)])
    return finish(sums, degree, features, w_self, w_neigh)


def solution(mesh):
    both = ("loop", "rep")
    return jax.shard_map(
        shards,
        mesh=mesh,
        in_specs=(P(both, None), P(both, None, None), P(both), P(both), P(both), P(both), P(), P()),
        out_specs=P(both, None),
        check_vma=False,
    )
```
